32 devices in a mesh: dp: 8 (over z, y), tensor: 4 (over x, core).
Axes of the slice: x: 2, y: 2, z: 4, core: 2. Of those that a mesh axis runs over, the one named last changes fastest.
Arguments:
- tokens: bfloat16 [2048, 1024], P('dp'), may hold values from -6 to 6
- norm_gain: float32 [1024], replicated, may hold values from 0.25 to 1.75
- w_query: bfloat16 [1024, 1024], P(None, 'tensor'), may hold values from -0.1875 to 0.1875
- w_key: bfloat16 [1024, 1024], P(None, 'tensor'), may hold values from -0.1875 to 0.1875
- w_value: bfloat16 [1024, 2048], P(None, 'tensor'), may hold values from -0.1875 to 0.1875
- w_outgate: bfloat16 [1024, 2048], P(None, 'tensor'), may hold values from -0.1875 to 0.1875
- w_decay: bfloat16 [1024, 8], P(None, 'tensor'), may hold values from -0.1875 to 0.1875
- w_beta: bfloat16 [1024, 8], P(None, 'tensor'), may hold values from -0.1875 to 0.1875
- conv_query: float32 [4, 1024], P(None, 'tensor'), may hold values from -3 to 3
- conv_key: float32 [4, 1024], P(None, 'tensor'), may hold values from -3 to 3
- conv_value: float32 [4, 2048], P(None, 'tensor'), may hold values from -3 to 3
- decay_log: float32 [8], P('tensor'), may hold values from -6 to 0.5
- decay_bias: float32 [8], P('tensor'), may hold values from -1 to 1
- out_norm_gain: float32 [256], replicated, may hold values from 0.25 to 1.75
- w_out: bfloat16 [1024, 2048], P(None, 'tensor'), may hold values from -0.125 to 0.125
- ffn_gain: float32 [1024], replicated, may hold values from 0.25 to 1.75
- w_gate: bfloat16 [1024, 2816], P(None, 'tensor'), may hold values from -0.1875 to 0.1875
- w_up: bfloat16 [1024, 2816], P(None, 'tensor'), may hold values from -0.1875 to 0.1875
- w_down: bfloat16 [1024, 2816], P(None, 'tensor'), may hold values from -0.109375 to 0.109375
- cotangent: bfloat16 [2048, 1024], P('dp'), may hold values from -6 to 6
Outputs:
- layer_out: float32 [2048, 1024], P('dp', 'tensor')
- grad_input: float32 [2048, 1024], P('dp', 'tensor')
- grad_norm_gain: float32 [1024], replicated
- grad_query: float32 [1024, 1024], P('dp', 'tensor')
- grad_key: float32 [1024, 1024], P('dp', 'tensor')
- grad_value: float32 [1024, 2048], P('dp', 'tensor')
- grad_outgate: float32 [1024, 2048], P('dp', 'tensor')
- grad_decay: float32 [1024, 8], P('dp', 'tensor')
- grad_beta: float32 [1024, 8], P('dp', 'tensor')
- grad_conv_query: float32 [4, 1024], P(None, 'tensor')
- grad_conv_key: float32 [4, 1024], P(None, 'tensor')
- grad_conv_value: float32 [4, 2048], P(None, 'tensor')
- grad_decay_log: float32 [8], P('tensor')
- grad_decay_bias: float32 [8], P('tensor')
- grad_out_norm_gain: float32 [256], replicated
- grad_out: float32 [1024, 2048], P('dp', 'tensor')
- grad_ffn_gain: float32 [1024], replicated
- grad_gate: float32 [1024, 2816], P('dp', 'tensor')
- grad_up: float32 [1024, 2816], P('dp', 'tensor')
- grad_down: float32 [1024, 2816], P('dp', 'tensor')
The draws below stay inside these ranges and needn't reach their ends.
All inputs are finite; a program needn't handle non-finite values.
Results may differ from the reference program's by a relative error of at most 0.012.
Values sent between devices are 32-bit elements; how exact they have to be, the bound alone decides.
No kernel may reach another device: no remote copies, remote signals or barrier semaphores. Data moves between devices by JAX's collectives and lax.ppermute only.
A program may use at most 128 MiB of HBM per device.

```python
import jax
import jax.numpy as jnp
from jax import lax

D = 1024
H = 8
DK = 128
DV = 256
FF = 2816
KCONV = 4
GROUP = 64
TOK_DEV = 256
TOKENS = 2048


def strengthened(drawn, own_key, source, target, blocks, factor):
    def block_of(axis_at):
        return (jnp.arange(drawn.shape[axis_at]) // (drawn.shape[axis_at] // blocks)).reshape((-1,) + (1,) * (drawn.ndim - 1 - axis_at))

    one_side = jax.random.permutation(own_key, blocks)[block_of(target)]
    second = (block_of(target) + blocks // 2) % blocks
    return jnp.where((block_of(source) == one_side) | (block_of(source) == second), factor * drawn, drawn)


def levels(stream_key, extent, pieces, smallest, largest):
    factor_of = 1.0
    for axis_at, parts in pieces:
        draws = jax.random.uniform(jax.random.fold_in(jax.random.fold_in(stream_key, 6), axis_at), (parts,), jnp.float32, smallest / len(pieces), largest / len(pieces))
        factor_of = factor_of * jnp.repeat(jnp.exp(draws), extent[axis_at] // parts).reshape((-1,) + (1,) * (len(extent) - 1 - axis_at))
    return factor_of


def bell_draw(own_key, shape, width, reach, split=(), held_as=jnp.bfloat16):
    loudness = levels(own_key, shape, split, -0.22, 0.18) if split else 1.0
    drawn = jax.random.normal(own_key, shape, jnp.float32) * width * loudness
    return jnp.minimum(jnp.maximum(drawn, -reach), reach).astype(held_as)


def gaussian_with(key, dims, scale, most, shards, heavy, held_as=jnp.bfloat16):
    values = scale * jax.random.normal(key, dims, jnp.float32)
    if shards:
        values = values * levels(key, dims, shards, -0.22, 0.18)
    return jnp.clip(strengthened(values, jax.random.fold_in(key, 3), *heavy), -most, most).astype(held_as)


def setup_inputs(seed: int = 0) -> dict:
    splits = jax.random.split(jax.random.key(seed), 21)
    return {
        "tokens": gaussian_with(splits[0], (TOKENS, D), 1.0, 6.0, ((0, 8),), (0, 1, 8, 2.0)),
        "norm_gain": jnp.clip(1.0 + 0.15 * jax.random.normal(splits[1], (D,), jnp.float32), 0.25, 1.75),
        "w_query": bell_draw(splits[2], (D, H * DK), D ** -0.5, 0.1875, ((1, 4),)),
        "w_key": bell_draw(splits[3], (D, H * DK), D ** -0.5, 0.1875, ((1, 4),)),
        "w_value": bell_draw(splits[4], (D, H * DV), D ** -0.5, 0.1875, ((1, 4),)),
        "w_outgate": bell_draw(splits[5], (D, H * DV), D ** -0.5, 0.1875, ((1, 4),)),
        "w_decay": bell_draw(splits[6], (D, H), D ** -0.5, 0.1875, ((1, 4),)),
        "w_beta": bell_draw(splits[7], (D, H), D ** -0.5, 0.1875, ((1, 4),)),
        "conv_query": bell_draw(splits[8], (KCONV, H * DK), 0.5, 3.0, ((1, 4),), jnp.float32),
        "conv_key": bell_draw(splits[9], (KCONV, H * DK), 0.5, 3.0, ((1, 4),), jnp.float32),
        "conv_value": bell_draw(splits[10], (KCONV, H * DV), 0.5, 3.0, ((1, 4),), jnp.float32),
        "decay_log": jnp.clip(-6.0 + 6.5 * jax.random.uniform(splits[11], (H,), jnp.float32) ** levels(splits[11], (H,), ((0, 4),), -0.2, 0.2), -6.0, 0.5),
        "decay_bias": jnp.clip(jax.random.uniform(splits[12], (H,), jnp.float32, -1.0, 1.0) * levels(splits[12], (H,), ((0, 4),), -0.4, 0.0), -1.0, 1.0),
        "out_norm_gain": jnp.clip(1.0 + 0.15 * jax.random.normal(splits[13], (DV,), jnp.float32), 0.25, 1.75),
        "w_out": bell_draw(splits[14], (D, H * DV), (H * DV) ** -0.5, 0.125, ((1, 4),)),
        "ffn_gain": jnp.clip(1.0 + 0.15 * jax.random.normal(splits[15], (D,), jnp.float32), 0.25, 1.75),
        "w_gate": bell_draw(splits[16], (D, FF), D ** -0.5, 0.1875, ((1, 4),)),
        "w_up": bell_draw(splits[17], (D, FF), D ** -0.5, 0.1875, ((1, 4),)),
        "w_down": bell_draw(splits[18], (D, FF), FF ** -0.5, 0.109375, ((1, 4),)),
        "cotangent": gaussian_with(splits[19], (TOKENS, D), 1.0, 6.0, ((0, 8),), (0, 1, 8, 2.0)),
    }


EPSILON = 1e-06
HIGH = lax.Precision.HIGHEST

def causal_conv(signal, taps):
    length = signal.shape[0]
    count = taps.shape[0]
    padded = jnp.concatenate([jnp.zeros((count - 1, signal.shape[1]), jnp.float32), signal], axis=0)
    total = taps[0] * padded[0:length]
    for index in range(1, count):
        total = total + taps[index] * padded[index:index + length]
    return total

def head_norm(signal, heads):
    shaped = signal.reshape(signal.shape[0], heads, -1)
    return shaped * lax.rsqrt(lax.optimization_barrier(jnp.sum(shaped * shaped, axis=2, keepdims=True)) + EPSILON)

def delta_rule(query, keys, values, beta, logdecay, block):
    length, heads, kdim = keys.shape
    vdim = values.shape[2]
    blocks = length // block
    position = jnp.arange(block)
    lower = (position[:, None] >= position[None, :])[:, :, None]
    strict = (position[:, None] > position[None, :])[:, :, None]
    identity = jnp.eye(block, dtype=jnp.float32)[None]
    squares = block.bit_length() - 2

    def step(state, inputs):
        qblk, kblk, vblk, bblk, gblk = inputs
        cumul = jnp.cumsum(gblk, axis=0)
        ratio = jnp.exp(jnp.where(lower, cumul[:, None, :] - cumul[None, :, :], -1e+30))
        growth = jnp.exp(cumul)
        tail = jnp.exp(cumul[-1][None, :] - cumul)
        keykey = jnp.einsum('thd,shd->tsh', kblk, kblk, precision=HIGH)
        strong = jnp.where(strict, keykey * ratio * bblk[:, None, :], 0.0)
        known = jnp.einsum('thd,hed->the', kblk, state, precision=HIGH)
        target = bblk[:, :, None] * (vblk - growth[:, :, None] * known)
        matrix = jnp.transpose(strong, (2, 0, 1))
        inverse = identity - matrix
        power = matrix
        for count in range(squares):
            power = jnp.einsum('hij,hjk->hik', power, power, precision=HIGH)
            inverse = jnp.einsum('hij,hjk->hik', inverse, identity + power, precision=HIGH)
        fresh = jnp.einsum('hts,she->hte', inverse, target, precision=HIGH)
        scores = jnp.where(lower, jnp.einsum('thd,shd->tsh', qblk, kblk, precision=HIGH) * ratio, 0.0)
        result = growth[:, :, None] * jnp.einsum('thd,hed->the', qblk, state, precision=HIGH)
        result = result + jnp.einsum('tsh,hse->the', scores, fresh, precision=HIGH)
        weighted = tail[:, :, None] * kblk
        new_state = growth[-1][:, None, None] * state + jnp.einsum('hse,shd->hed', fresh, weighted, precision=HIGH)
        return (new_state, result)
    start = jnp.zeros((heads, vdim, kdim), jnp.float32)
    inputs = (query.reshape(blocks, block, heads, kdim), keys.reshape(blocks, block, heads, kdim), values.reshape(blocks, block, heads, vdim), beta.reshape(blocks, block, heads), logdecay.reshape(blocks, block, heads))
    final, results = lax.scan(step, start, inputs)
    return results.reshape(length, heads * vdim)

def mixer(qlin, klin, vlin, alin, blin, conv_q, conv_k, conv_v, rate_log, rate_bias):
    heads = rate_log.shape[0]
    length = qlin.shape[0]
    kdim = qlin.shape[1] // heads
    query = head_norm(jax.nn.silu(causal_conv(qlin, conv_q)), heads) * kdim ** (-0.5)
    keys = head_norm(jax.nn.silu(causal_conv(klin, conv_k)), heads)
    values = jax.nn.silu(causal_conv(vlin, conv_v)).reshape(length, heads, -1)
    beta = jax.nn.sigmoid(blin)
    logdecay = -jnp.exp(rate_log) * jax.nn.softplus(alin + rate_bias)
    return delta_rule(query, keys, values, beta, logdecay, GROUP)

def gated_norm(mixed, zlin, gain):
    length = mixed.shape[0]
    vdim = gain.shape[0]
    shaped = mixed.reshape(length, -1, vdim)
    scale = lax.rsqrt(lax.optimization_barrier(jnp.mean(shaped * shaped, axis=2, keepdims=True)) + EPSILON)
    gates = jax.nn.silu(zlin).reshape(length, -1, vdim)
    return (shaped * scale * gain * gates).reshape(length, -1)

def rms_back(grad_normed, unit, inverse_rms, gain):
    scaled = grad_normed * gain
    return inverse_rms * (scaled - unit * lax.optimization_barrier(jnp.mean(scaled * unit, axis=1, keepdims=True)))

def mat(operand, weights):
    return jnp.dot(operand, weights, preferred_element_type=jnp.float32)

def one_sequence(params, seq_tokens, seq_cot):
    norm_gain, w_query, w_key, w_value, w_outgate, w_decay, w_beta, conv_query, conv_key, conv_value, decay_log, decay_bias, out_norm_gain, w_out, ffn_gain, w_gate, w_up, w_down = params
    inputs = seq_tokens.astype(jnp.float32)
    inv_first = lax.rsqrt(lax.optimization_barrier(jnp.mean(inputs * inputs, axis=1, keepdims=True)) + EPSILON)
    unit_first = inputs * inv_first
    normed_first = (unit_first * norm_gain).astype(jnp.bfloat16)
    qlin = mat(normed_first, w_query)
    klin = mat(normed_first, w_key)
    vlin = mat(normed_first, w_value)
    zlin = mat(normed_first, w_outgate)
    alin = mat(normed_first, w_decay)
    blin = mat(normed_first, w_beta)
    mixed, mixer_back = jax.vjp(mixer, qlin, klin, vlin, alin, blin, conv_query, conv_key, conv_value, decay_log, decay_bias)
    gated, gated_back = jax.vjp(gated_norm, mixed, zlin, out_norm_gain)
    gated_bf = gated.astype(jnp.bfloat16)
    resid = inputs + mat(gated_bf, w_out.T)
    inv_second = lax.rsqrt(lax.optimization_barrier(jnp.mean(resid * resid, axis=1, keepdims=True)) + EPSILON)
    unit_second = resid * inv_second
    normed_second = (unit_second * ffn_gain).astype(jnp.bfloat16)
    glin = mat(normed_second, w_gate)
    ulin = mat(normed_second, w_up)
    sigm = jax.nn.sigmoid(glin)
    silu_gate = glin * sigm
    hidden = (silu_gate * ulin).astype(jnp.bfloat16)
    layer_rows = resid + mat(hidden, w_down.T)
    dhidden = mat(seq_cot, w_down)
    grad_down = mat(seq_cot.T, hidden)
    dglin = (dhidden * ulin * sigm * (1.0 + glin * (1.0 - sigm))).astype(jnp.bfloat16)
    dulin = (dhidden * silu_gate).astype(jnp.bfloat16)
    grad_gate = mat(normed_second.T, dglin)
    grad_up = mat(normed_second.T, dulin)
    dnormed2 = mat(dglin, w_gate.T) + mat(dulin, w_up.T)
    grad_ffn_gain = lax.optimization_barrier(jnp.sum(dnormed2 * unit_second, axis=0))
    dresid = seq_cot.astype(jnp.float32) + rms_back(dnormed2, unit_second, inv_second, ffn_gain)
    dresid_bf = dresid.astype(jnp.bfloat16)
    grad_out = mat(dresid_bf.T, gated_bf)
    dgated = mat(dresid_bf, w_out)
    dmixed, dzlin, grad_out_norm = gated_back(dgated)
    dqlin, dklin, dvlin, dalin, dblin, grad_cq, grad_ck, grad_cv, grad_dlog, grad_dbias = mixer_back(dmixed)
    dq_bf = dqlin.astype(jnp.bfloat16)
    dk_bf = dklin.astype(jnp.bfloat16)
    dv_bf = dvlin.astype(jnp.bfloat16)
    dz_bf = dzlin.astype(jnp.bfloat16)
    da_bf = dalin.astype(jnp.bfloat16)
    db_bf = dblin.astype(jnp.bfloat16)
    normed_t = normed_first.T
    grad_query = mat(normed_t, dq_bf)
    grad_key = mat(normed_t, dk_bf)
    grad_value = mat(normed_t, dv_bf)
    grad_outgate = mat(normed_t, dz_bf)
    grad_decay = mat(normed_t, da_bf)
    grad_beta = mat(normed_t, db_bf)
    dnormed1 = mat(dq_bf, w_query.T) + mat(dk_bf, w_key.T) + mat(dv_bf, w_value.T) + mat(dz_bf, w_outgate.T) + mat(da_bf, w_decay.T) + mat(db_bf, w_beta.T)
    grad_norm_gain = lax.optimization_barrier(jnp.sum(dnormed1 * unit_first, axis=0))
    grad_rows = dresid + rms_back(dnormed1, unit_first, inv_first, norm_gain)
    grads = (grad_norm_gain, grad_query, grad_key, grad_value, grad_outgate, grad_decay, grad_beta, grad_cq, grad_ck, grad_cv, grad_dlog, grad_dbias, grad_out_norm, grad_out, grad_ffn_gain, grad_gate, grad_up, grad_down)
    return ((layer_rows, grad_rows), grads)

def reference(tokens, norm_gain, w_query, w_key, w_value, w_outgate, w_decay, w_beta, conv_query, conv_key, conv_value, decay_log, decay_bias, out_norm_gain, w_out, ffn_gain, w_gate, w_up, w_down, cotangent):
    params = (norm_gain, w_query, w_key, w_value, w_outgate, w_decay, w_beta, conv_query, conv_key, conv_value, decay_log, decay_bias, out_norm_gain, w_out, ffn_gain, w_gate, w_up, w_down)

    def step(totals, pair):
        rows, grads = one_sequence(params, pair[0], pair[1])
        return (jax.tree.map(jnp.add, totals, grads), rows)
    zeros = tuple((jnp.zeros(param.shape, jnp.float32) for param in params))
    seqs_tok = tokens.reshape(-1, TOK_DEV, D)
    seqs_cot = cotangent.reshape(-1, TOK_DEV, D)
    totals, (layer_rows, grad_rows) = lax.scan(step, zeros, (seqs_tok, seqs_cot))
    return (layer_rows.reshape(TOKENS, D), grad_rows.reshape(TOKENS, D), totals[0], totals[1], totals[2], totals[3], totals[4], totals[5], totals[6], totals[7], totals[8], totals[9], totals[10], totals[11], totals[12], totals[13], totals[14], totals[15], totals[16], totals[17])
```

```python
import functools

import jax
import jax.numpy as jnp
from jax import lax
from jax.experimental import pallas as pl
from jax.experimental.pallas import tpu as pltpu
from jax.sharding import PartitionSpec as P

EPSILON = 1e-06
F32 = jnp.float32
BF16 = jnp.bfloat16
HIGH = lax.Precision.HIGHEST
LANES = 128
BASE = 16


def mm(a, b, ca=1, cb=0):
    return lax.dot_general(a, b, (((ca,), (cb,)), ((), ())), preferred_element_type=F32)


def split(x):
    high = x.astype(BF16)
    return high, (x - high.astype(F32)).astype(BF16)


def mm3(a, b, ca=1, cb=0):
    return mm(a[0], b[0], ca, cb) + (mm(a[0], b[1], ca, cb) + mm(a[1], b[0], ca, cb))


def iotas(n):
    return (
        lax.broadcasted_iota(jnp.int32, (n, n), 0),
        lax.broadcasted_iota(jnp.int32, (n, n), 1),
    )


def sigmoid(x):
    return 1.0 / (1.0 + jnp.exp(-x))


def softplus(x):
    return jnp.maximum(x, 0.0) + jnp.log1p(jnp.exp(-jnp.abs(x)))


def shifted(x, by):
    if by == 0:
        return x
    length = x.shape[0]
    position = lax.broadcasted_iota(jnp.int32, x.shape, 0)
    inside = position >= by if by > 0 else position < length + by
    return jnp.where(inside, pltpu.roll(x, by % length, 0), 0.0)


def conv(x, taps):
    count = taps.shape[0]
    total = taps[0:1] * shifted(x, count - 1)
    for index in range(1, count):
        total = total + taps[index : index + 1] * shifted(x, count - 1 - index)
    return total


def conv_back(grad, x, taps):
    count = taps.shape[0]
    total, rows = None, []
    for index in range(count):
        by = count - 1 - index
        rows.append(jnp.sum(grad * shifted(x, by), axis=0, keepdims=True))
        term = taps[index : index + 1] * shifted(grad, -by)
        total = term if total is None else total + term
    return total, rows


def unit_lower_inverse(strong, row, col):
    size = strong.shape[0]
    base = min(BASE, size)
    eye = jnp.where(row == col, 1.0, 0.0)
    power = jnp.where(row // base == col // base, -strong, 0.0)
    inverse = eye + power
    done = 2
    while done < base:
        pieces = split(power)
        power = mm3(pieces, pieces)
        inverse = inverse + mm3(split(inverse), split(power))
        done *= 2
    block = base
    while block < size:
        cross = (row // (2 * block) == col // (2 * block)) & (row // block > col // block)
        pieces = split(inverse)
        middle = mm3(split(jnp.where(cross, strong, 0.0)), pieces)
        inverse = inverse - mm3(pieces, split(middle))
        block *= 2
    return inverse


def head_unit(x):
    return lax.rsqrt(jnp.sum(x * x, axis=1, keepdims=True) + EPSILON)


def front_kernel(
    heads,
    tok,
    cot,
    gain,
    w_q,
    w_k,
    w_v,
    w_z,
    w_ab,
    w_abt,
    cq,
    ck,
    cv,
    rate_row,
    bias_row,
    rate_col,
    bias_col,
    out_gain,
    w_out,
    part,
    normed_out,
    cot_out,
    q_out,
    k_out,
    v_out,
    z_out,
    ab_out,
    mixed_out,
    gated_out,
    ratio_out,
    known_out,
    score_out,
    inverse_out,
    fresh_out,
):
    x = tok[...].astype(F32)
    length = x.shape[0]
    inv = lax.rsqrt(jnp.mean(x * x, axis=1, keepdims=True) + EPSILON)
    normed = ((x * inv) * gain[...]).astype(BF16)
    normed_out[...] = normed.astype(F32)
    cot_out[...] = cot[...].astype(F32)
    ab = mm(normed, w_ab[...])
    ab_t = mm(w_abt[...], normed, 1, 1)
    ab_out[...] = ab
    qlin = mm(normed, w_q[...])
    klin = mm(normed, w_k[...])
    vlin = mm(normed, w_v[...])
    zlin = mm(normed, w_z[...])
    q_out[...] = qlin
    k_out[...] = klin
    v_out[...] = vlin
    z_out[...] = zlin
    row, col = iotas(length)
    lower = row >= col
    strict = row > col
    tri = jnp.where(lower, 1.0, 0.0)
    decay = -jnp.exp(rate_row[...]) * softplus(ab + bias_row[...])
    decay_t = -jnp.exp(rate_col[...]) * softplus(ab_t + bias_col[...])
    cumul = jnp.dot(tri, decay, precision=HIGH, preferred_element_type=F32)
    cumul_t = lax.dot_general(
        decay_t, tri, (((1,), (1,)), ((), ())), precision=HIGH, preferred_element_type=F32
    )
    beta_all = sigmoid(ab)
    qpre = conv(qlin, cq[...])
    kpre = conv(klin, ck[...])
    vpre = conv(vlin, cv[...])
    qact = qpre * sigmoid(qpre)
    kact = kpre * sigmoid(kpre)
    vact = vpre * sigmoid(vpre)
    gates = zlin * sigmoid(zlin)
    kdim = qlin.shape[1] // heads
    vdim = vlin.shape[1] // heads
    gated = []
    for head in range(heads):
        kspan = slice(head * kdim, (head + 1) * kdim)
        vspan = slice(head * vdim, (head + 1) * vdim)
        qh, kh = qact[:, kspan], kact[:, kspan]
        query = split(qh * head_unit(qh) * kdim ** (-0.5))
        keys = split(kh * head_unit(kh))
        beta = beta_all[:, heads + head : heads + head + 1]
        gap = cumul[:, head : head + 1] - cumul_t[head : head + 1, :]
        ratio = jnp.exp(jnp.where(lower, jnp.where(row == col, 0.0, gap), -1e30))
        known = jnp.where(strict, mm3(keys, keys, 1, 1) * ratio, 0.0)
        score = jnp.where(lower, mm3(query, keys, 1, 1) * ratio, 0.0)
        inverse = unit_lower_inverse(known * beta, row, col)
        fresh = mm3(split(inverse), split(beta * vact[:, vspan]))
        mixed = mm3(split(score), split(fresh))
        scale = lax.rsqrt(jnp.mean(mixed * mixed, axis=1, keepdims=True) + EPSILON)
        gated.append((mixed * scale * out_gain[...] * gates[:, vspan]).astype(BF16))
        mixed_out[:, vspan] = mixed
        gated_out[:, vspan] = gated[head].astype(F32)
        ratio_out[head] = ratio
        known_out[head] = known
        score_out[head] = score
        inverse_out[head] = inverse
        fresh_out[head] = fresh
    total = None
    for head in range(heads):
        term = mm(gated[head], w_out[:, head * vdim : (head + 1) * vdim], 1, 1)
        total = term if total is None else total + term
    part[...] = total


def ffn_kernel(
    tok, mixer, gain, w_gate, w_up, dhid, w_down, resid_out, normed_out, second, hid_out, dg_out, du_out, ffn
):
    resid = tok[...].astype(F32) + mixer[...]
    resid_out[...] = resid
    inv = lax.rsqrt(jnp.mean(resid * resid, axis=1, keepdims=True) + EPSILON)
    normed = ((resid * inv) * gain[...]).astype(BF16)
    normed_out[...] = normed.astype(F32)
    glin = mm(normed, w_gate[...])
    ulin = mm(normed, w_up[...])
    sigm = sigmoid(glin)
    silu = glin * sigm
    hidden = (silu * ulin).astype(BF16)
    dhidden = dhid[...]
    dglin = (dhidden * ulin * sigm * (1.0 + glin * (1.0 - sigm))).astype(BF16)
    dulin = (dhidden * silu).astype(BF16)
    second[...] = mm(dglin, w_gate[...], 1, 1) + mm(dulin, w_up[...], 1, 1)
    hid_out[...] = hidden.astype(F32)
    dg_out[...] = dglin.astype(F32)
    du_out[...] = dulin.astype(F32)
    ffn[...] = mm(hidden, w_down[...], 1, 1)


def middle_kernel(
    heads, cot, dnormed_in, resid_in, gain, w_out, mixed, zlin, out_gain, dresid_out, narrow_out, dz_out, dmixed_out, fg_out, og_out
):
    resid = resid_in[...]
    dnormed = dnormed_in[...]
    inv = lax.rsqrt(jnp.mean(resid * resid, axis=1, keepdims=True) + EPSILON)
    unit = resid * inv
    fg_out[...] = jnp.sum(dnormed * unit, axis=0, keepdims=True)
    scaled = dnormed * gain[...]
    dresid = cot[...].astype(F32) + inv * (
        scaled - unit * jnp.mean(scaled * unit, axis=1, keepdims=True)
    )
    dresid_out[...] = dresid
    narrow = dresid.astype(BF16)
    narrow_out[...] = narrow.astype(F32)
    dgated_all = mm(narrow, w_out[...])
    vdim = mixed.shape[1] // heads
    total = None
    for head in range(heads):
        span = slice(head * vdim, (head + 1) * vdim)
        mix, z, dgated = mixed[:, span], zlin[:, span], dgated_all[:, span]
        scale = lax.rsqrt(jnp.mean(mix * mix, axis=1, keepdims=True) + EPSILON)
        sigm = sigmoid(z)
        gates = z * sigm
        unit_mix = mix * scale
        pulled = dgated * gates
        term = jnp.sum(pulled * unit_mix, axis=0, keepdims=True)
        total = term if total is None else total + term
        dunit = pulled * out_gain[...]
        dmixed_out[:, span] = scale * (
            dunit - unit_mix * jnp.mean(dunit * unit_mix, axis=1, keepdims=True)
        )
        dgate = dgated * (unit_mix * out_gain[...])
        dz_out[:, span] = (dgate * (sigm + gates * (1.0 - sigm))).astype(BF16).astype(F32)
    og_out[...] = total


def back_kernel(
    heads,
    shards,
    tok,
    gain,
    w_q,
    w_k,
    w_v,
    w_z,
    w_ab,
    cq,
    ck,
    cv,
    rate_row,
    bias_row,
    qlin_in,
    klin_in,
    vlin_in,
    ab_in,
    ratio_in,
    known_in,
    score_in,
    inverse_in,
    fresh_in,
    dmixed_in,
    dz_in,
    first,
    rows_out,
    norm_out,
    dq_out,
    dk_out,
    dv_out,
    dab_out,
    conv_q_out,
    conv_k_out,
    conv_v_out,
    rates_out,
):
    length = tok.shape[0]
    row, col = iotas(length)
    lower = row >= col
    strict = row > col
    upper = jnp.where(col >= row, 1.0, 0.0).astype(BF16)
    ab = ab_in[...]
    beta_all = sigmoid(ab)
    qlin, klin, vlin = qlin_in[...], klin_in[...], vlin_in[...]
    qpre, kpre, vpre = conv(qlin, cq[...]), conv(klin, ck[...]), conv(vlin, cv[...])
    qsig, ksig, vsig = sigmoid(qpre), sigmoid(kpre), sigmoid(vpre)
    qact, kact, vact = qpre * qsig, kpre * ksig, vpre * vsig
    kdim = qlin.shape[1] // heads
    vdim = vlin.shape[1] // heads
    lane = lax.broadcasted_iota(jnp.int32, ab.shape, 1)
    dgamma = jnp.zeros_like(ab)
    dbeta_all = jnp.zeros_like(ab)
    dqs, dks, dvs = [], [], []
    for head in range(heads):
        kspan = slice(head * kdim, (head + 1) * kdim)
        vspan = slice(head * vdim, (head + 1) * vdim)
        qh, kh, value = qact[:, kspan], kact[:, kspan], vact[:, vspan]
        qinv, kinv = head_unit(qh), head_unit(kh)
        qunit, kunit = qh * qinv, kh * kinv
        query, keys = split(qunit * kdim ** (-0.5)), split(kunit)
        beta = beta_all[:, heads + head : heads + head + 1]
        ratio, known, score = ratio_in[head], known_in[head], score_in[head]
        fresh = split(fresh_in[head])
        dmixed = split(dmixed_in[:, vspan])
        dscore = jnp.where(lower, mm3(dmixed, fresh, 1, 1), 0.0)
        dfresh = mm3(split(score), dmixed, 0, 0)
        dtarget = mm3(split(inverse_in[head]), split(dfresh), 0, 0)
        dstrong = jnp.where(strict, -mm3(split(dtarget), fresh, 1, 1), 0.0)
        dbeta = jnp.sum(dstrong * known, axis=1, keepdims=True) + jnp.sum(
            dtarget * value, axis=1, keepdims=True
        )
        dknown = dstrong * beta
        flow = dknown * known + dscore * score
        pieces = split(flow)
        below = mm(upper, pieces[0]) + mm(upper, pieces[1])
        ddecay = jnp.sum(jnp.where(strict, below, 0.0), axis=1, keepdims=True)
        dgamma = dgamma + jnp.where(lane == head, ddecay, 0.0)
        dbeta_all = dbeta_all + jnp.where(lane == heads + head, dbeta, 0.0)
        dkk = split(dknown * ratio)
        dqk = split(dscore * ratio)
        dkeys = mm3(dkk, keys) + mm3(dkk, keys, 0, 0) + mm3(dqk, query, 0, 0)
        dquery = mm3(dqk, keys) * kdim ** (-0.5)
        dqs.append(qinv * (dquery - qunit * jnp.sum(dquery * qunit, axis=1, keepdims=True)))
        dks.append(kinv * (dkeys - kunit * jnp.sum(dkeys * kunit, axis=1, keepdims=True)))
        dvs.append(dtarget * beta)
    dqpre = jnp.concatenate(dqs, axis=1) * (qsig + qact * (1.0 - qsig))
    dkpre = jnp.concatenate(dks, axis=1) * (ksig + kact * (1.0 - ksig))
    dvpre = jnp.concatenate(dvs, axis=1) * (vsig + vact * (1.0 - vsig))
    dq, rows_q = conv_back(dqpre, qlin, cq[...])
    dk, rows_k = conv_back(dkpre, klin, ck[...])
    dv, rows_v = conv_back(dvpre, vlin, cv[...])
    for index in range(len(rows_q)):
        conv_q_out[index : index + 1, :] = rows_q[index]
        conv_k_out[index : index + 1, :] = rows_k[index]
        conv_v_out[index : index + 1, :] = rows_v[index]
    rate = -jnp.exp(rate_row[...])
    da = dgamma * rate * sigmoid(ab + bias_row[...])
    db = dbeta_all * beta_all * (1.0 - beta_all)
    dlog = jnp.sum(dgamma * rate * softplus(ab + bias_row[...]), axis=0, keepdims=True)
    rates_out[0:1, :] = dlog
    rates_out[1:2, :] = jnp.sum(da, axis=0, keepdims=True)
    dab = (da + db).astype(BF16)
    dq, dk, dv = dq.astype(BF16), dk.astype(BF16), dv.astype(BF16)
    dq_out[...] = dq.astype(F32)
    dk_out[...] = dk.astype(F32)
    dv_out[...] = dv.astype(F32)
    dab_out[...] = dab.astype(F32)
    total = mm(dq, w_q[...], 1, 1) + mm(dk, w_k[...], 1, 1)
    total = total + mm(dv, w_v[...], 1, 1) + mm(dz_in[...].astype(BF16), w_z[...], 1, 1)
    total = total + mm(dab, w_ab[...], 1, 1)
    width = total.shape[1] // shards
    for index in range(shards):
        first[index] = total[:, index * width : (index + 1) * width]
    x = tok[...].astype(F32)
    unit = x * lax.rsqrt(jnp.mean(x * x, axis=1, keepdims=True) + EPSILON)
    product = total * unit
    norm_out[...] = jnp.sum(product, axis=0, keepdims=True)
    pieces = split(product * gain[...])
    ones = jnp.full((8, total.shape[1]), 1.0, BF16)
    rows_out[...] = mm(ones, pieces[0], 1, 1) + mm(ones, pieces[1], 1, 1)


def outer_kernel(own, other, grads, far, keep, send):
    here, there = grads[...].astype(BF16), far[...].astype(BF16)
    half = keep.shape[0]
    for span, out in ((slice(half, 2 * half), send), (slice(0, half), keep)):
        out[...] = mm(own[:, span].astype(BF16), here, 0, 0) + mm(
            other[:, span].astype(BF16), there, 0, 0
        )


VMEM_SPEC = pl.BlockSpec(memory_space=pltpu.VMEM)


def call(kernel, name, outs, *args):
    shapes = tuple(jax.ShapeDtypeStruct(shape, kind) for shape, kind in outs)
    return pl.pallas_call(
        kernel,
        out_shape=shapes,
        in_specs=[VMEM_SPEC] * len(args),
        out_specs=tuple([VMEM_SPEC] * len(shapes)),
        name=name,
    )(*args)


def bits_of(axis):
    size = lax.axis_size(axis)
    return size.bit_length() - 1


def swap(x, axis, bit):
    size = lax.axis_size(axis)
    return lax.ppermute(x, axis, [(i, i ^ (1 << bit)) for i in range(size)])


def butterfly(x, axis):
    for bit in range(bits_of(axis)):
        x = x + swap(x, axis, bit)
    return x


def pick(x, index):
    return lax.dynamic_index_in_dim(x, index, 0, keepdims=False)


def sum_over(x, axis):
    bits = bits_of(axis)
    rows, width = x.shape
    mine = lax.axis_index(axis) & 1
    halves = x.reshape(2, rows // 2, width)
    total = pick(halves, mine) + swap(pick(halves, 1 - mine), axis, 0)
    for bit in range(1, bits):
        total = total + swap(total, axis, bit)
    other = swap(total, axis, 0)
    low = jnp.where(mine == 0, total, other)
    high = jnp.where(mine == 0, other, total)
    return jnp.concatenate([low, high], axis=0)


def scatter_over(x, axis):
    me = lax.axis_index(axis)
    for bit in range(bits_of(axis)):
        pairs = x.reshape((x.shape[0] // 2, 2) + x.shape[1:])
        mine = (me >> bit) & 1
        keep = lax.dynamic_index_in_dim(pairs, mine, 1, keepdims=False)
        send = lax.dynamic_index_in_dim(pairs, 1 - mine, 1, keepdims=False)
        x = keep + swap(send, axis, bit)
    return x[0]


def relative(x, axis):
    size = lax.axis_size(axis)
    bits = bits_of(axis)
    me = lax.axis_index(axis)
    block = x.shape[1] // size
    blocks = []
    for place in range(size):
        index = sum(((place >> bit) & 1) << (bits - 1 - bit) for bit in range(bits))
        blocks.append(lax.dynamic_slice_in_dim(x, (me ^ index) * block, block, 1))
    half = size // 2
    return jnp.concatenate(blocks[:half], axis=1), jnp.concatenate(blocks[half:], axis=1)


class Rows:
    def __init__(self, x, axis):
        self.axis = axis
        self.own, send = relative(x, axis)
        self.other = swap(send, axis, 0)

    def gradient(self, name, grads):
        far = swap(grads, self.axis, 0)
        half = self.own.shape[1] // 2
        width = grads.shape[1]
        keep, send = call(
            outer_kernel,
            name,
            (((half, width), F32), ((half, width), F32)),
            self.own,
            self.other,
            grads,
            far,
        )
        bits = bits_of(self.axis)
        for bit in range(1, bits):
            come = swap(send, self.axis, bit)
            if bit == bits - 1:
                return keep + come
            half //= 2
            keep, send = keep[:half] + come[:half], keep[half:] + come[half:]


def local(
    tokens,
    norm_gain,
    w_query,
    w_key,
    w_value,
    w_outgate,
    w_decay,
    w_beta,
    conv_query,
    conv_key,
    conv_value,
    decay_log,
    decay_bias,
    out_norm_gain,
    w_out,
    ffn_gain,
    w_gate,
    w_up,
    w_down,
    cotangent,
):
    length, width = tokens.shape
    heads = decay_log.shape[0]
    shards = lax.axis_size("tensor")
    kwidth, vwidth = w_query.shape[1], w_value.shape[1]
    fwidth = w_gate.shape[1]
    vdim = vwidth // heads
    rank = lax.axis_index("tensor")
    share = width // shards

    both = jnp.concatenate([w_decay, w_beta], axis=1)
    w_ab = jnp.pad(both, ((0, 0), (0, LANES - 2 * heads)))
    w_abt = jnp.pad(both.T, ((0, 8 - 2 * heads), (0, 0)))
    rate_row = jnp.pad(decay_log[None], ((0, 0), (0, LANES - heads)))
    bias_row = jnp.pad(decay_bias[None], ((0, 0), (0, LANES - heads)))
    rate_col = jnp.pad(decay_log[:, None], ((0, 8 - heads), (0, 0)))
    bias_col = jnp.pad(decay_bias[:, None], ((0, 8 - heads), (0, 0)))
    gain_row, ffn_row, out_row = norm_gain[None], ffn_gain[None], out_norm_gain[None]

    square = ((heads, length, length), F32)
    (
        part,
        normed_first,
        wide_cot,
        qlin,
        klin,
        vlin,
        zlin,
        ab,
        mixed,
        gated,
        ratio,
        known,
        score,
        inverse,
        fresh,
    ) = call(
        functools.partial(front_kernel, heads),
        "front",
        (
            ((length, width), F32),
            ((length, width), F32),
            ((length, width), F32),
            ((length, kwidth), F32),
            ((length, kwidth), F32),
            ((length, vwidth), F32),
            ((length, vwidth), F32),
            ((length, LANES), F32),
            ((length, vwidth), F32),
            ((length, vwidth), F32),
            square,
            square,
            square,
            square,
            ((heads, length, vdim), F32),
        ),
        tokens,
        cotangent,
        gain_row,
        w_query,
        w_key,
        w_value,
        w_outgate,
        w_ab,
        w_abt,
        conv_query,
        conv_key,
        conv_value,
        rate_row,
        bias_row,
        rate_col,
        bias_col,
        out_row,
        w_out,
    )
    mixer = sum_over(part, "tensor")
    rows_first = Rows(normed_first, "dp")
    rows_cot = Rows(wide_cot, "dp")
    dhidden = jnp.dot(cotangent, w_down, preferred_element_type=F32)
    resid, normed_second, second_part, hidden, dglin, dulin, ffn_part = call(
        ffn_kernel,
        "ffn",
        (
            ((length, width), F32),
            ((length, width), F32),
            ((length, width), F32),
            ((length, fwidth), F32),
            ((length, fwidth), F32),
            ((length, fwidth), F32),
            ((length, width), F32),
        ),
        tokens,
        mixer,
        ffn_row,
        w_gate,
        w_up,
        dhidden,
        w_down,
    )
    dnormed2 = sum_over(second_part, "tensor")
    rows_second = Rows(normed_second, "dp")
    sum_gate = rows_second.gradient("outer_gate", dglin)
    sum_up = rows_second.gradient("outer_up", dulin)
    sum_down = rows_cot.gradient("outer_down", hidden)
    ffn_share = scatter_over(
        jnp.swapaxes(ffn_part.reshape(length, shards, share), 0, 1), "tensor"
    )
    layer_out = lax.dynamic_slice_in_dim(resid, rank * share, share, 1) + ffn_share
    dresid, dresid_narrow, dz, dmixed, grad_ffn_gain, grad_out_norm = call(
        functools.partial(middle_kernel, heads),
        "middle",
        (
            ((length, width), F32),
            ((length, width), F32),
            ((length, vwidth), F32),
            ((length, vwidth), F32),
            ((1, width), F32),
            ((1, vdim), F32),
        ),
        cotangent,
        dnormed2,
        resid,
        ffn_row,
        w_out,
        mixed,
        zlin,
        out_row,
    )
    rows_dresid = Rows(dresid_narrow, "dp")
    sum_out = rows_dresid.gradient("outer_out", gated)
    sum_outgate = rows_first.gradient("outer_gates", dz)
    (
        first,
        row_sums,
        grad_norm_gain,
        dq,
        dk,
        dv,
        dab,
        grad_cq,
        grad_ck,
        grad_cv,
        rates,
    ) = call(
        functools.partial(back_kernel, heads, shards),
        "back",
        (
            ((shards, length, share), F32),
            ((8, length), F32),
            ((1, width), F32),
            ((length, kwidth), F32),
            ((length, kwidth), F32),
            ((length, vwidth), F32),
            ((length, LANES), F32),
            (conv_query.shape, F32),
            (conv_key.shape, F32),
            (conv_value.shape, F32),
            ((2, LANES), F32),
        ),
        tokens,
        gain_row,
        w_query,
        w_key,
        w_value,
        w_outgate,
        w_ab,
        conv_query,
        conv_key,
        conv_value,
        rate_row,
        bias_row,
        qlin,
        klin,
        vlin,
        ab,
        ratio,
        known,
        score,
        inverse,
        fresh,
        dmixed,
        dz,
    )
    sum_qkv = rows_first.gradient("outer_qkv", jnp.concatenate([dq, dk, dv], axis=1))
    grad_ab = lax.dot_general(
        dab[:, : 2 * heads],
        normed_first,
        (((0,), (0,)), ((), ())),
        preferred_element_type=F32,
    )
    dnormed_share = scatter_over(first, "tensor")
    shared = jnp.concatenate(
        [row_sums[0], grad_norm_gain[0], grad_out_norm[0]]
    ).reshape(-1, LANES)
    shared = butterfly(shared, "tensor").reshape(-1)
    row_total = shared[:length]
    norm_parts = shared[length:]
    flat = jnp.concatenate(
        [
            norm_parts,
            grad_ffn_gain[0],
            grad_cq.reshape(-1),
            grad_ck.reshape(-1),
            grad_cv.reshape(-1),
            rates.reshape(-1),
            grad_ab.reshape(-1),
        ]
    ).reshape(-1, LANES)
    flat = butterfly(flat, "dp").reshape(-1)
    pieces, at = [], 0
    for shape in (
        (width,),
        (vdim,),
        (width,),
        conv_query.shape,
        conv_key.shape,
        conv_value.shape,
        (2, LANES),
        (2 * heads, width),
    ):
        count = 1
        for extent in shape:
            count *= extent
        pieces.append(flat[at : at + count].reshape(shape))
        at += count
    sum_norm_gain, sum_out_norm, sum_ffn_gain, sum_cq, sum_ck, sum_cv, sum_rates, sum_ab = pieces
    block = width // lax.axis_size("dp")
    own_ab = lax.dynamic_slice_in_dim(sum_ab, lax.axis_index("dp") * block, block, 1).T

    inputs = tokens.astype(F32)
    inv_first = lax.rsqrt(jnp.mean(inputs * inputs, axis=1, keepdims=True) + EPSILON)
    offset = rank * share
    unit_share = lax.dynamic_slice_in_dim(inputs, offset, share, 1) * inv_first
    scaled = dnormed_share * lax.dynamic_slice_in_dim(norm_gain, offset, share, 0)[None]
    grad_input = lax.dynamic_slice_in_dim(dresid, offset, share, 1) + inv_first * (
        scaled - unit_share * (row_total / width)[:, None]
    )
    return (
        layer_out,
        grad_input,
        sum_norm_gain,
        sum_qkv[:, :kwidth],
        sum_qkv[:, kwidth : 2 * kwidth],
        sum_qkv[:, 2 * kwidth :],
        sum_outgate,
        own_ab[:, :heads],
        own_ab[:, heads:],
        sum_cq,
        sum_ck,
        sum_cv,
        sum_rates[0, :heads],
        sum_rates[1, :heads],
        sum_out_norm,
        sum_out,
        sum_ffn_gain,
        sum_gate,
        sum_up,
        sum_down,
    )


def solution(mesh):
    columns = P(None, "tensor")
    tokens = P("dp", None)
    spread = P("dp", "tensor")
    return jax.shard_map(
        local,
        mesh=mesh,
        in_specs=(
            tokens,
            P(),
            *([columns] * 9),
            P("tensor"),
            P("tensor"),
            P(),
            columns,
            P(),
            columns,
            columns,
            columns,
            tokens,
        ),
        out_specs=(
            spread,
            spread,
            P(),
            *([spread] * 6),
            columns,
            columns,
            columns,
            P("tensor"),
            P("tensor"),
            P(),
            spread,
            P(),
            spread,
            spread,
            spread,
        ),
        check_vma=False,
    )
```

```python
import functools

import jax
import jax.numpy as jnp
from jax import lax
from jax.experimental import pallas as pl
from jax.experimental.pallas import tpu as pltpu
from jax.sharding import PartitionSpec as P

EPSILON = 1e-06
F32 = jnp.float32
BF16 = jnp.bfloat16
HIGH = lax.Precision.HIGHEST
LANES = 128
SLOTS = 8
BASE = 16


def mm(a, b, ca=1, cb=0):
    return lax.dot_general(a, b, (((ca,), (cb,)), ((), ())), preferred_element_type=F32)


def split(x):
    high = x.astype(BF16)
    return high, (x - high.astype(F32)).astype(BF16)


def mm3(a, b, ca=1, cb=0):
    return mm(a[0], b[0], ca, cb) + (mm(a[0], b[1], ca, cb) + mm(a[1], b[0], ca, cb))


def iotas(n):
    return (
        lax.broadcasted_iota(jnp.int32, (n, n), 0),
        lax.broadcasted_iota(jnp.int32, (n, n), 1),
    )


def sigmoid(x):
    return 1.0 / (1.0 + jnp.exp(-x))


def softplus(x):
    return jnp.maximum(x, 0.0) + jnp.log1p(jnp.exp(-jnp.abs(x)))


def shifted(x, by):
    if by == 0:
        return x
    length = x.shape[0]
    position = lax.broadcasted_iota(jnp.int32, x.shape, 0)
    inside = position >= by if by > 0 else position < length + by
    return jnp.where(inside, pltpu.roll(x, by % length, 0), 0.0)


def conv(x, taps):
    count = taps.shape[0]
    total = taps[0:1] * shifted(x, count - 1)
    for index in range(1, count):
        total = total + taps[index : index + 1] * shifted(x, count - 1 - index)
    return total


def conv_back(grad, x, taps):
    count = taps.shape[0]
    total, rows = None, []
    for index in range(count):
        by = count - 1 - index
        rows.append(jnp.sum(grad * shifted(x, by), axis=0, keepdims=True))
        term = taps[index : index + 1] * shifted(grad, -by)
        total = term if total is None else total + term
    return total, rows


def unit_lower_inverse(strong, row, col):
    size = strong.shape[0]
    base = min(BASE, size)
    eye = jnp.where(row == col, 1.0, 0.0)
    power = jnp.where(row // base == col // base, -strong, 0.0)
    inverse = eye + power
    done = 2
    while done < base:
        pieces = split(power)
        power = mm3(pieces, pieces)
        inverse = inverse + mm3(split(inverse), split(power))
        done *= 2
    block = base
    while block < size:
        cross = (row // (2 * block) == col // (2 * block)) & (row // block > col // block)
        pieces = split(inverse)
        middle = mm3(split(jnp.where(cross, strong, 0.0)), pieces)
        inverse = inverse - mm3(pieces, split(middle))
        block *= 2
    return inverse


def head_unit(x):
    return lax.rsqrt(jnp.sum(x * x, axis=1, keepdims=True) + EPSILON)


def order_of(bits):
    count = len(bits)
    return [
        sum(((place >> (count - 1 - k)) & 1) << bits[k] for k in range(count))
        for place in range(1 << count)
    ]


def relative_blocks(blocks, index):
    bit = 0
    while (1 << bit) < len(blocks):
        flag = ((index >> bit) & 1) == 1
        blocks = [jnp.where(flag, blocks[j ^ (1 << bit)], blocks[j]) for j in range(len(blocks))]
        bit += 1
    return blocks


def emit(x, index, bits, refs):
    if len(refs) == 1:
        refs[0][...] = x
        return
    order = order_of(bits)
    block = x.shape[1] // len(order)
    blocks = relative_blocks(
        [x[:, j * block : (j + 1) * block] for j in range(len(order))], index
    )
    half = len(order) // 2
    for place, j in enumerate(order):
        at = (place % half) * block
        refs[place // half][:, at : at + block] = blocks[j]


def emit_shards(x, index, bits, keep, send):
    order = order_of(bits)
    block = x.shape[1] // len(order)
    blocks = relative_blocks(
        [x[:, j * block : (j + 1) * block] for j in range(len(order))], index
    )
    half = len(order) // 2
    for place, j in enumerate(order):
        (keep, send)[place // half][place % half] = blocks[j]


def rows_in(scratch, mine, own, other):
    half = own.shape[0]
    scratch[pl.ds(pl.multiple_of(mine * half, half), half), :] = own
    scratch[pl.ds(pl.multiple_of((1 - mine) * half, half), half), :] = other


def rows_out_of(scratch, mine, keep, send):
    half = keep.shape[0]
    keep[...] = scratch[pl.ds(pl.multiple_of(mine * half, half), half), :]
    send[...] = scratch[pl.ds(pl.multiple_of((1 - mine) * half, half), half), :]


def scalar_rows(ref, heads, axis):
    shape = (1, SLOTS) if axis == 1 else (SLOTS, 1)
    place = lax.broadcasted_iota(jnp.int32, shape, axis)
    total = jnp.zeros(shape, F32)
    for head in range(heads):
        total = jnp.where(place == head, ref[head], total)
    return total


def gate_weights(scratch, w_decay, w_beta):
    heads = w_decay.shape[0]
    scratch[...] = jnp.zeros_like(scratch)
    scratch[0:heads, :] = w_decay[...].astype(F32)
    scratch[heads : 2 * heads, :] = w_beta[...].astype(F32)
    return scratch[...].astype(BF16)


def front_kernel(
    heads, bits, pair, place, rate_log, rate_bias, tok, cot, gain, w_q, w_k, w_v, w_z, w_decay, w_beta,
    cq, ck, cv, out_gain, w_out, *rest
):
    keep, send = rest[0], rest[1]
    normed_refs, cot_refs = rest[2 : 2 + pair], rest[2 + pair : 2 + 2 * pair]
    (
        q_out, k_out, v_out, z_out, ab_out, mixed_out, gated_out, ratio_out, known_out, score_out,
        inverse_out, fresh_out, gate_scratch, part,
    ) = rest[2 + 2 * pair :]
    x = tok[...].astype(F32)
    length = x.shape[0]
    inv = lax.rsqrt(jnp.mean(x * x, axis=1, keepdims=True) + EPSILON)
    normed = ((x * inv) * gain[...]).astype(BF16)
    w_ab = gate_weights(gate_scratch, w_decay, w_beta)
    ab = mm(normed, w_ab, 1, 1)
    ab_t = mm(w_ab, normed, 1, 1)
    ab_out[...] = ab
    qlin = mm(normed, w_q[...])
    klin = mm(normed, w_k[...])
    vlin = mm(normed, w_v[...])
    zlin = mm(normed, w_z[...])
    q_out[...] = qlin
    k_out[...] = klin
    v_out[...] = vlin
    z_out[...] = zlin
    row, col = iotas(length)
    lower = row >= col
    strict = row > col
    tri = jnp.where(lower, 1.0, 0.0)
    decay = -jnp.exp(scalar_rows(rate_log, heads, 1)) * softplus(ab + scalar_rows(rate_bias, heads, 1))
    decay_t = -jnp.exp(scalar_rows(rate_log, heads, 0)) * softplus(
        ab_t + scalar_rows(rate_bias, heads, 0)
    )
    cumul = jnp.dot(tri, decay, precision=HIGH, preferred_element_type=F32)
    cumul_t = lax.dot_general(
        decay_t, tri, (((1,), (1,)), ((), ())), precision=HIGH, preferred_element_type=F32
    )
    beta_all = sigmoid(ab)
    qpre = conv(qlin, cq[...])
    kpre = conv(klin, ck[...])
    vpre = conv(vlin, cv[...])
    qact = qpre * sigmoid(qpre)
    kact = kpre * sigmoid(kpre)
    vact = vpre * sigmoid(vpre)
    gates = zlin * sigmoid(zlin)
    kdim = qlin.shape[1] // heads
    vdim = vlin.shape[1] // heads
    gated = []
    for head in range(heads):
        kspan = slice(head * kdim, (head + 1) * kdim)
        vspan = slice(head * vdim, (head + 1) * vdim)
        qh, kh = qact[:, kspan], kact[:, kspan]
        query = split(qh * head_unit(qh) * kdim ** (-0.5))
        keys = split(kh * head_unit(kh))
        beta = beta_all[:, heads + head : heads + head + 1]
        gap = cumul[:, head : head + 1] - cumul_t[head : head + 1, :]
        ratio = jnp.exp(jnp.where(lower, jnp.where(row == col, 0.0, gap), -1e30))
        known = jnp.where(strict, mm3(keys, keys, 1, 1) * ratio, 0.0)
        score = jnp.where(lower, mm3(query, keys, 1, 1) * ratio, 0.0)
        inverse = unit_lower_inverse(known * beta, row, col)
        fresh = mm3(split(inverse), split(beta * vact[:, vspan]))
        mixed = mm3(split(score), split(fresh))
        scale = lax.rsqrt(jnp.mean(mixed * mixed, axis=1, keepdims=True) + EPSILON)
        gated.append((mixed * scale * out_gain[...] * gates[:, vspan]).astype(BF16))
        mixed_out[:, vspan] = mixed
        gated_out[:, vspan] = gated[head].astype(F32)
        ratio_out[head] = ratio
        known_out[head] = known
        score_out[head] = score
        inverse_out[head] = inverse
        fresh_out[head] = fresh
    total = None
    for head in range(heads):
        term = mm(gated[head], w_out[:, head * vdim : (head + 1) * vdim], 1, 1)
        total = term if total is None else total + term
    part[...] = total
    rows_out_of(part, place[1] & 1, keep, send)
    emit(normed.astype(F32), place[0], bits, normed_refs)
    emit(cot[...].astype(F32), place[0], bits, cot_refs)


def ffn_kernel(
    bits, pair, place, tok, own, other, gain, w_gate, w_up, w_down, cot, keep, send, resid_out, hid_out, dg_out, du_out, *rest
):
    normed_refs, work = rest[:pair], rest[pair]
    mine = place[1] & 1
    rows_in(work, mine, own[...], other[...])
    resid = tok[...].astype(F32) + work[...]
    resid_out[...] = resid
    inv = lax.rsqrt(jnp.mean(resid * resid, axis=1, keepdims=True) + EPSILON)
    normed = ((resid * inv) * gain[...]).astype(BF16)
    dhidden = mm(w_down[...], cot[...], 1, 1)
    glin = mm(w_gate[...], normed, 1, 1)
    ulin = mm(w_up[...], normed, 1, 1)
    sigm = sigmoid(glin)
    silu = glin * sigm
    dglin = (dhidden * ulin * sigm * (1.0 + glin * (1.0 - sigm))).astype(BF16)
    dulin = (dhidden * silu).astype(BF16)
    work[...] = mm(dglin, w_gate[...], 0, 0) + mm(dulin, w_up[...], 0, 0)
    rows_out_of(work, mine, keep, send)
    hid_out[...] = (silu * ulin).astype(BF16).astype(F32)
    dg_out[...] = dglin.astype(F32)
    du_out[...] = dulin.astype(F32)
    emit(normed.astype(F32), place[0], bits, normed_refs)


def down_kernel(bits, place, hidden, w_down, keep, send):
    emit_shards(mm(hidden[...].astype(BF16), w_down[...], 0, 0), place[1], bits, keep, send)


def middle_kernel(
    heads, bits, pair, place, cot, own, other, resid_in, gain, w_out, mixed, zlin, out_gain,
    dresid_out, dz_out, dmixed_out, fg_out, og_out, *rest
):
    narrow_refs, work = rest[:pair], rest[pair]
    rows_in(work, place[1] & 1, own[...], other[...])
    resid = resid_in[...]
    dnormed = work[...]
    inv = lax.rsqrt(jnp.mean(resid * resid, axis=1, keepdims=True) + EPSILON)
    unit = resid * inv
    fg_out[...] = jnp.sum(dnormed * unit, axis=0, keepdims=True)
    scaled = dnormed * gain[...]
    dresid = cot[...].astype(F32) + inv * (
        scaled - unit * jnp.mean(scaled * unit, axis=1, keepdims=True)
    )
    dresid_out[...] = dresid
    narrow = dresid.astype(BF16)
    emit(narrow.astype(F32), place[0], bits, narrow_refs)
    dgated_all = mm(narrow, w_out[...])
    vdim = mixed.shape[1] // heads
    total = None
    for head in range(heads):
        span = slice(head * vdim, (head + 1) * vdim)
        mix, z, dgated = mixed[:, span], zlin[:, span], dgated_all[:, span]
        scale = lax.rsqrt(jnp.mean(mix * mix, axis=1, keepdims=True) + EPSILON)
        sigm = sigmoid(z)
        gates = z * sigm
        unit_mix = mix * scale
        pulled = dgated * gates
        term = jnp.sum(pulled * unit_mix, axis=0, keepdims=True)
        total = term if total is None else total + term
        dunit = pulled * out_gain[...]
        dmixed_out[:, span] = scale * (
            dunit - unit_mix * jnp.mean(dunit * unit_mix, axis=1, keepdims=True)
        )
        dgate = dgated * (unit_mix * out_gain[...])
        dz_out[:, span] = (dgate * (sigm + gates * (1.0 - sigm))).astype(BF16).astype(F32)
    og_out[...] = total


def back_kernel(
    heads, bits, place, rate_log, rate_bias, tok, gain, w_q, w_k, w_v, w_z, w_decay, w_beta, cq, ck, cv,
    qlin_in, klin_in, vlin_in, ab_in, ratio_in, known_in, score_in, inverse_in, fresh_in, dmixed_in, dz_in,
    fg_in, og_in, keep, send, grads_out, small_out, gate_scratch
):
    length, width = tok.shape
    row, col = iotas(length)
    lower = row >= col
    strict = row > col
    upper = jnp.where(col >= row, 1.0, 0.0).astype(BF16)
    ab = ab_in[...]
    beta_all = sigmoid(ab)
    qlin, klin, vlin = qlin_in[...], klin_in[...], vlin_in[...]
    qpre, kpre, vpre = conv(qlin, cq[...]), conv(klin, ck[...]), conv(vlin, cv[...])
    qsig, ksig, vsig = sigmoid(qpre), sigmoid(kpre), sigmoid(vpre)
    qact, kact, vact = qpre * qsig, kpre * ksig, vpre * vsig
    kwidth, vwidth = qlin.shape[1], vlin.shape[1]
    kdim = kwidth // heads
    vdim = vwidth // heads
    lane = lax.broadcasted_iota(jnp.int32, ab.shape, 1)
    dgamma = jnp.zeros_like(ab)
    dbeta_all = jnp.zeros_like(ab)
    dqs, dks, dvs = [], [], []
    for head in range(heads):
        kspan = slice(head * kdim, (head + 1) * kdim)
        vspan = slice(head * vdim, (head + 1) * vdim)
        qh, kh, value = qact[:, kspan], kact[:, kspan], vact[:, vspan]
        qinv, kinv = head_unit(qh), head_unit(kh)
        qunit, kunit = qh * qinv, kh * kinv
        query, keys = split(qunit * kdim ** (-0.5)), split(kunit)
        beta = beta_all[:, heads + head : heads + head + 1]
        ratio, known, score = ratio_in[head], known_in[head], score_in[head]
        fresh = split(fresh_in[head])
        dmixed = split(dmixed_in[:, vspan])
        dscore = jnp.where(lower, mm3(dmixed, fresh, 1, 1), 0.0)
        dfresh = mm3(split(score), dmixed, 0, 0)
        dtarget = mm3(split(inverse_in[head]), split(dfresh), 0, 0)
        dstrong = jnp.where(strict, -mm3(split(dtarget), fresh, 1, 1), 0.0)
        dbeta = jnp.sum(dstrong * known, axis=1, keepdims=True) + jnp.sum(
            dtarget * value, axis=1, keepdims=True
        )
        dknown = dstrong * beta
        flow = dknown * known + dscore * score
        pieces = split(flow)
        below = mm(upper, pieces[0]) + mm(upper, pieces[1])
        ddecay = jnp.sum(jnp.where(strict, below, 0.0), axis=1, keepdims=True)
        dgamma = dgamma + jnp.where(lane == head, ddecay, 0.0)
        dbeta_all = dbeta_all + jnp.where(lane == heads + head, dbeta, 0.0)
        dkk = split(dknown * ratio)
        dqk = split(dscore * ratio)
        dkeys = mm3(dkk, keys) + mm3(dkk, keys, 0, 0) + mm3(dqk, query, 0, 0)
        dquery = mm3(dqk, keys) * kdim ** (-0.5)
        dqs.append(qinv * (dquery - qunit * jnp.sum(dquery * qunit, axis=1, keepdims=True)))
        dks.append(kinv * (dkeys - kunit * jnp.sum(dkeys * kunit, axis=1, keepdims=True)))
        dvs.append(dtarget * beta)
    dqpre = jnp.concatenate(dqs, axis=1) * (qsig + qact * (1.0 - qsig))
    dkpre = jnp.concatenate(dks, axis=1) * (ksig + kact * (1.0 - ksig))
    dvpre = jnp.concatenate(dvs, axis=1) * (vsig + vact * (1.0 - vsig))
    dq, rows_q = conv_back(dqpre, qlin, cq[...])
    dk, rows_k = conv_back(dkpre, klin, ck[...])
    dv, rows_v = conv_back(dvpre, vlin, cv[...])
    rate = -jnp.exp(scalar_rows(rate_log, heads, 1))
    shifted_ab = ab + scalar_rows(rate_bias, heads, 1)
    da = dgamma * rate * sigmoid(shifted_ab)
    db = dbeta_all * beta_all * (1.0 - beta_all)
    dlog = jnp.sum(dgamma * rate * softplus(shifted_ab), axis=0, keepdims=True)
    dab = (da + db).astype(BF16)
    dq, dk, dv = dq.astype(BF16), dk.astype(BF16), dv.astype(BF16)
    grads_out[:, 0:kwidth] = dq.astype(F32)
    grads_out[:, kwidth : 2 * kwidth] = dk.astype(F32)
    grads_out[:, 2 * kwidth :] = dv.astype(F32)
    w_ab = gate_weights(gate_scratch, w_decay, w_beta)
    total = mm(dq, w_q[...], 1, 1) + mm(dk, w_k[...], 1, 1)
    total = total + mm(dv, w_v[...], 1, 1) + mm(dz_in[...].astype(BF16), w_z[...], 1, 1)
    total = total + mm(dab, w_ab)
    emit_shards(total, place[1], bits, keep, send)
    x = tok[...].astype(F32)
    unit = x * lax.rsqrt(jnp.mean(x * x, axis=1, keepdims=True) + EPSILON)
    product = total * unit
    pieces = split(product * gain[...])
    ones = jnp.full((8, width), 1.0, BF16)
    small_out[...] = jnp.zeros_like(small_out)
    row_sums = mm(ones, pieces[0], 1, 1) + mm(ones, pieces[1], 1, 1)
    small_out[0:1, 0:length] = row_sums[0:1]
    small_out[1:2, :] = jnp.sum(product, axis=0, keepdims=True)
    small_out[2:3, 0:vdim] = og_in[...]
    small_out[8:9, :] = fg_in[...]
    small_out[9:10, 0:SLOTS] = dlog
    small_out[10:11, 0:SLOTS] = jnp.sum(da, axis=0, keepdims=True)
    taps = cq.shape[0]
    for index in range(taps):
        at = 11 + index
        small_out[at : at + 1, 0:kwidth] = rows_q[index]
        small_out[at : at + 1, kwidth : 2 * kwidth] = rows_k[index]
        small_out[at : at + 1, 2 * kwidth : 2 * kwidth + vwidth] = rows_v[index]
    at = 11 + taps
    normed = (unit * gain[...]).astype(BF16)
    small_out[at : at + SLOTS, :] = mm(dab, normed, 0, 0)


def outer_kernel(own, other, grads, far, keep, send):
    here, there = grads[...].astype(BF16), far[...].astype(BF16)
    half = keep.shape[0]
    for span, out in ((slice(half, 2 * half), send), (slice(0, half), keep)):
        out[...] = mm(own[:, span].astype(BF16), here, 0, 0) + mm(
            other[:, span].astype(BF16), there, 0, 0
        )


def outer_kernel_t(own, other, grads, far, keep, send):
    here, there = grads[...].astype(BF16), far[...].astype(BF16)
    half = keep.shape[1]
    for span, out in ((slice(half, 2 * half), send), (slice(0, half), keep)):
        out[...] = mm(here, own[:, span].astype(BF16)) + mm(there, other[:, span].astype(BF16))


VMEM_SPEC = pl.BlockSpec(memory_space=pltpu.VMEM)
SMEM_SPEC = pl.BlockSpec(memory_space=pltpu.SMEM)


def call(kernel, name, outs, *args, scalars=0, scratch=()):
    shapes = tuple(jax.ShapeDtypeStruct(shape, F32) for shape in outs)
    return pl.pallas_call(
        kernel,
        out_shape=shapes,
        in_specs=[SMEM_SPEC] * scalars + [VMEM_SPEC] * (len(args) - scalars),
        out_specs=tuple([VMEM_SPEC] * len(shapes)),
        scratch_shapes=[pltpu.VMEM(shape, F32) for shape in scratch],
        name=name,
    )(*args)


def bits_of(axis):
    size = lax.axis_size(axis)
    return size.bit_length() - 1


def swap(x, axis, bit):
    size = lax.axis_size(axis)
    return lax.ppermute(x, axis, [(i, i ^ (1 << bit)) for i in range(size)])


def butterfly(x, axis):
    for bit in range(bits_of(axis)):
        x = x + swap(x, axis, bit)
    return x


def sum_halves(keep, send, axis):
    total = keep + swap(send, axis, 0)
    for bit in range(1, bits_of(axis)):
        total = total + swap(total, axis, bit)
    return total, swap(total, axis, 0)


def scatter_rest(keep, send, axis, bits):
    total = keep + swap(send, axis, bits[0])
    for bit in bits[1:]:
        half = total.shape[0] // 2
        total = total[:half] + swap(total[half:], axis, bit)
    return total[0]


def arranged(outs, axis, bits):
    if len(outs) == 2:
        return outs
    (x,) = outs
    me = lax.axis_index(axis)
    order = order_of(bits)
    block = x.shape[1] // len(order)
    blocks = [lax.dynamic_slice_in_dim(x, (me ^ j) * block, block, 1) for j in order]
    half = len(order) // 2
    return jnp.concatenate(blocks[:half], axis=1), jnp.concatenate(blocks[half:], axis=1)


class Rows:
    def __init__(self, outs, axis, bits):
        self.axis, self.bits = axis, bits
        self.own, send = arranged(outs, axis, bits)
        self.other = swap(send, axis, bits[0])

    def far(self, grads):
        return swap(grads, self.axis, self.bits[0])

    def gradient(self, name, grads, far=None, turned=False):
        far = self.far(grads) if far is None else far
        half = self.own.shape[1] // 2
        shape = (grads.shape[0], half) if turned else (half, grads.shape[1])
        keep, send = call(
            outer_kernel_t if turned else outer_kernel,
            name,
            (shape, shape),
            self.own,
            self.other,
            grads,
            far,
        )
        axis = 1 if turned else 0
        for bit in self.bits[1:]:
            come = swap(send, self.axis, bit)
            if bit == self.bits[-1]:
                return keep + come
            half //= 2

            def first(x):
                return lax.slice_in_dim(x, 0, half, axis=axis)

            def second(x):
                return lax.slice_in_dim(x, half, 2 * half, axis=axis)

            keep, send = first(keep) + first(come), second(keep) + second(come)


def local(
    tokens, norm_gain, w_query, w_key, w_value, w_outgate, w_decay, w_beta, conv_query, conv_key, conv_value,
    decay_log, decay_bias, out_norm_gain, w_out, ffn_gain, w_gate, w_up, w_down, cotangent
):
    length, width = tokens.shape
    heads = decay_log.shape[0]
    shards = lax.axis_size("tensor")
    members = lax.axis_size("dp")
    kwidth, vwidth = w_query.shape[1], w_value.shape[1]
    fwidth = w_gate.shape[1]
    vdim = vwidth // heads
    rank = lax.axis_index("tensor")
    share = width // shards
    block = width // members
    place = jnp.stack([lax.axis_index("dp"), rank]).astype(jnp.int32)
    near = list(range(bits_of("dp")))
    far = [near[1], near[0]] + near[2:]
    across = list(range(bits_of("tensor")))
    pair = 2 if block % LANES == 0 else 1
    spread = [(length, width // 2)] * 2 if pair == 2 else [(length, width)]

    w_decay_t, w_beta_t = w_decay.T, w_beta.T
    w_gate_t, w_up_t, w_down_t = w_gate.T, w_up.T, w_down.T
    gain_row, ffn_row, out_row = norm_gain[None], ffn_gain[None], out_norm_gain[None]

    halves = [(length // 2, width)] * 2
    square = (heads, length, length)
    outs = call(
        functools.partial(front_kernel, heads, far, pair),
        "front",
        [
            *halves,
            *spread,
            *spread,
            (length, kwidth),
            (length, kwidth),
            (length, vwidth),
            (length, vwidth),
            (length, SLOTS),
            (length, vwidth),
            (length, vwidth),
            square,
            square,
            square,
            square,
            (heads, length, vdim),
        ],
        place, decay_log, decay_bias, tokens, cotangent, gain_row, w_query, w_key, w_value, w_outgate,
        w_decay_t, w_beta_t, conv_query, conv_key, conv_value, out_row, w_out,
        scalars=3,
        scratch=((SLOTS, width), (length, width)),
    )
    keep, send = outs[:2]
    normed_first, wide_cot = outs[2 : 2 + pair], outs[2 + pair : 2 + 2 * pair]
    (qlin, klin, vlin, zlin, ab, mixed, gated, ratio, known, score, inverse, fresh) = outs[2 + 2 * pair :]
    own, other = sum_halves(keep, send, "tensor")
    rows_first = Rows(normed_first, "dp", far)
    rows_cot = Rows(wide_cot, "dp", far)
    gated_far = swap(gated, "dp", near[0])
    turned = (fwidth, length)
    outs = call(
        functools.partial(ffn_kernel, near, pair),
        "ffn",
        [*halves, (length, width), turned, turned, turned, *spread],
        place, tokens, own, other, ffn_row, w_gate_t, w_up_t, w_down_t, cotangent,
        scalars=1,
        scratch=((length, width),),
    )
    keep, send, resid, hidden, dglin, dulin = outs[:6]
    own, other = sum_halves(keep, send, "tensor")
    rows_second = Rows(outs[6:], "dp", near)
    sum_down = rows_cot.gradient("outer_down", hidden, turned=True)
    sum_gate = rows_second.gradient("outer_gate", dglin, turned=True)
    sum_up = rows_second.gradient("outer_up", dulin, turned=True)
    shard_halves = [(shards // 2, length, share)] * 2
    ffn_share = scatter_rest(
        *call(
            functools.partial(down_kernel, across), "down", shard_halves, place, hidden, w_down_t, scalars=1
        ),
        "tensor",
        across,
    )
    layer_out = lax.dynamic_slice_in_dim(resid, rank * share, share, 1) + ffn_share
    outs = call(
        functools.partial(middle_kernel, heads, near, pair),
        "middle",
        [(length, width), (length, vwidth), (length, vwidth), (1, width), (1, vdim), *spread],
        place, cotangent, own, other, resid, ffn_row, w_out, mixed, zlin, out_row,
        scalars=1,
        scratch=((length, width),),
    )
    dresid, dz, dmixed, grad_ffn_gain, grad_out_norm = outs[:5]
    rows_dresid = Rows(outs[5:], "dp", near)
    sum_outgate = rows_first.gradient("outer_outgate", dz)
    sum_out = rows_dresid.gradient("outer_out", gated, gated_far)
    taps = conv_query.shape[0]
    tall = -(-(11 + taps + SLOTS) // 8) * 8
    keep, send, grads_qkv, small = call(
        functools.partial(back_kernel, heads, across),
        "back",
        [*shard_halves, (length, 2 * kwidth + vwidth), (tall, width)],
        place, decay_log, decay_bias, tokens, gain_row, w_query, w_key, w_value, w_outgate,
        w_decay_t, w_beta_t, conv_query, conv_key, conv_value,
        qlin, klin, vlin, ab, ratio, known, score, inverse, fresh, dmixed, dz, grad_ffn_gain, grad_out_norm,
        scalars=3,
        scratch=((SLOTS, width),),
    )
    sum_qkv = rows_first.gradient("outer_qkv", grads_qkv)
    dnormed_share = scatter_rest(keep, send, "tensor", across)
    shared = butterfly(small[:8], "tensor")
    row_total = shared[0, :length]
    small = butterfly(jnp.concatenate([shared, small[8:]], axis=0), "dp")
    sum_taps = small[11 : 11 + taps]
    at = 11 + taps
    own_ab = lax.dynamic_slice_in_dim(
        small[at : at + 2 * heads], lax.axis_index("dp") * block, block, 1
    ).T

    inputs = tokens.astype(F32)
    inv_first = lax.rsqrt(jnp.mean(inputs * inputs, axis=1, keepdims=True) + EPSILON)
    offset = rank * share
    unit_share = lax.dynamic_slice_in_dim(inputs, offset, share, 1) * inv_first
    scaled = dnormed_share * lax.dynamic_slice_in_dim(norm_gain, offset, share, 0)[None]
    grad_input = lax.dynamic_slice_in_dim(dresid, offset, share, 1) + inv_first * (
        scaled - unit_share * (row_total / width)[:, None]
    )
    return (
        layer_out,
        grad_input,
        small[1],
        sum_qkv[:, :kwidth],
        sum_qkv[:, kwidth : 2 * kwidth],
        sum_qkv[:, 2 * kwidth :],
        sum_outgate,
        own_ab[:, :heads],
        own_ab[:, heads:],
        sum_taps[:, :kwidth],
        sum_taps[:, kwidth : 2 * kwidth],
        sum_taps[:, 2 * kwidth : 2 * kwidth + vwidth],
        small[9, :heads],
        small[10, :heads],
        small[2, :vdim],
        sum_out,
        small[8],
        sum_gate.T,
        sum_up.T,
        sum_down.T,
    )


def solution(mesh):
    columns = P(None, "tensor")
    tokens = P("dp", None)
    spread = P("dp", "tensor")
    return jax.shard_map(
        local,
        mesh=mesh,
        in_specs=(
            tokens,
            P(),
            *([columns] * 9),
            P("tensor"),
            P("tensor"),
            P(),
            columns,
            P(),
            columns,
            columns,
            columns,
            tokens,
        ),
        out_specs=(
            spread,
            spread,
            P(),
            *([spread] * 6),
            columns,
            columns,
            columns,
            P("tensor"),
            P("tensor"),
            P(),
            spread,
            P(),
            spread,
            spread,
            spread,
        ),
        check_vma=False,
    )
```
